128 devices in a mesh: grp: 8 (over z, core), sub: 16 (over y, x).
Axes of the slice: x: 4, y: 4, z: 4, core: 2. Of those that a mesh axis runs over, the one named last changes fastest.
Arguments:
- activations: bfloat16 [196608, 2048], P(('grp', 'sub')), may hold values from -16 to 16, as said below
- cotangent: bfloat16 [196608, 1024], P(('grp', 'sub')), may hold values from -16 to 16, as said below
- weight: bfloat16 [2048, 1024], replicated, may hold values from -0.125 to 0.125
- master: float32 [2048, 1024], P(('grp', 'sub')), may hold values from -1.5 to 1.5
- momentum: float32 [2048, 1024], P(('grp', 'sub')), may hold values from -6 to 6
Outputs:
- input_grad: bfloat16 [196608, 2048], P(('grp', 'sub'))
- new_momentum: float32 [2048, 1024], P(('grp', 'sub'))
- new_master: float32 [2048, 1024], P(('grp', 'sub'))
- new_weight: bfloat16 [2048, 1024], replicated
The draws below stay inside these ranges and needn't reach their ends.
Inputs may be any that keep to these rules, and one draw needn't show every extreme that they name: `activations`: activations of the kind a projection receives. `cotangent`: gradients of the kind a loss gives.
All inputs are finite; a program needn't handle non-finite values.
Results may differ from the reference program's by a relative error of at most 0.001.
Values may be sent and summed in bfloat16 or wider, within the bound.
A program may use at most 128 MiB of HBM per device.

```python
import jax
import jax.numpy as jnp
from jax import lax

D = 2048
KV = 1024
TOK_DEV = 1536
N_GRP = 8
N_SUB = 16


def shaped_draw(key, width, tag):
    group_rows = TOK_DEV * N_SUB
    base_key = jax.random.fold_in(key, tag)
    common = jax.random.normal(jax.random.fold_in(base_key, 1), (group_rows, width), jnp.float32)
    spread = jnp.exp(jax.random.uniform(jax.random.fold_in(base_key, 4), (width,), jnp.float32, jnp.log(0.3), jnp.log(3.0)))
    noise = jax.random.normal(jax.random.fold_in(base_key, 2), (N_GRP, group_rows, width), jnp.float32)
    weights = jax.random.uniform(jax.random.fold_in(base_key, 3), (N_GRP, 1, 1), jnp.float32, 0.6, 1.4)
    steps = jnp.arange(N_GRP, dtype=jnp.float32) / max(N_GRP - 1, 1)
    rising = (0.2 * jnp.power(3.0, steps))[:, None, None]
    ramp = jnp.power(3.0, jnp.arange(width, dtype=jnp.float32) / width)
    values = (weights * common[None] + rising * noise) * (spread * ramp)
    values = jnp.clip(values, -16.0, 16.0)
    return values.reshape(N_GRP * group_rows, width).astype(jnp.bfloat16)


def draw_activations(key, part):
    return shaped_draw(key, D, 11)


def draw_cotangent(key, part):
    return shaped_draw(key, KV, 23)


def block_scale(key, dims, shards, low, high):
    loudness = 1.0
    for axis_at, shards_of in shards:
        heights = jax.random.uniform(jax.random.fold_in(jax.random.fold_in(key, 6), axis_at), (shards_of,), jnp.float32, low / len(shards), high / len(shards))
        loudness = loudness * jnp.repeat(jnp.exp(heights), dims[axis_at] // shards_of).reshape((-1,) + (1,) * (len(dims) - 1 - axis_at))
    return loudness


def scatter_about(own_key, extent, deviation, reach, split=(), kind=jnp.bfloat16):
    factor_of = block_scale(own_key, extent, split, -0.22, 0.18) if split else 1.0
    array = jax.random.normal(own_key, extent, jnp.float32) * deviation * factor_of
    return jnp.minimum(jnp.maximum(array, -reach), reach).astype(kind)


def setup_inputs(seed: int = 0) -> dict:
    arg_keys = jax.random.split(jax.random.key(seed), 6)
    activations = draw_activations(jax.random.fold_in(arg_keys[5], 71), 0)
    cotangent = draw_cotangent(jax.random.fold_in(arg_keys[5], 71), 0)
    weight = scatter_about(arg_keys[2], (D, KV), D ** -0.5, 0.125)
    master = scatter_about(arg_keys[3], (D, KV), 0.1, 1.5, ((0, 128),), jnp.float32)
    momentum = scatter_about(arg_keys[4], (D, KV), 1.0, 6.0, ((0, 128),), jnp.float32)
    return dict(activations=activations, cotangent=cotangent, weight=weight, master=master, momentum=momentum)


def adasum_pair(lower, upper):
    lower_sq = jnp.sum(lower * lower)
    upper_sq = jnp.sum(upper * upper)
    cross = jnp.sum(lower * upper)
    return (1.0 - cross / (2.0 * (lower_sq + 1e-6))) * lower + (1.0 - cross / (2.0 * (upper_sq + 1e-6))) * upper


def reference(activations, cotangent, weight, master, momentum):
    group_rows = TOK_DEV * N_SUB
    scale = 1.0 / (group_rows ** 0.5)
    acts = activations.reshape(N_GRP, group_rows, D)
    cots = cotangent.reshape(N_GRP, group_rows, KV)

    def back_input(cot):
        return lax.dot_general(cot, weight, (((1,), (1,)), ((), ())), preferred_element_type=jnp.float32).astype(jnp.bfloat16)

    input_grad = lax.map(back_input, cots).reshape(N_GRP * group_rows, D)

    def back_weight(pair):
        return lax.dot_general(pair[0], pair[1], (((0,), (0,)), ((), ())), preferred_element_type=jnp.float32) * scale

    grads = lax.map(back_weight, (acts, cots))
    nodes = [grads[index] for index in range(N_GRP)]
    while len(nodes) > 1:
        nodes = [adasum_pair(nodes[2 * index], nodes[2 * index + 1]) for index in range(len(nodes) // 2)]
    combined = nodes[0]
    new_momentum = 0.9 * momentum + combined
    new_master = master - 0.05 * new_momentum
    new_weight = new_master.astype(jnp.bfloat16)
    return input_grad, new_momentum, new_master, new_weight
```

```python
import functools
import math

import jax
import jax.numpy as jnp
from jax import lax
from jax.experimental import pallas as pl
from jax.experimental.pallas import tpu as pltpu
from jax.sharding import PartitionSpec as P

MESH = pl.DeviceIdType.MESH
N = 8
LAG2, LAG3, LAG4, LAG5 = 1, 3, 4, 5
PARTS = ((0, 384, "zxy"), (384, 384, "xyz"), (768, 256, "yzx"))
PAIRS = [(i, j) for i in range(N) for j in range(i, N)]


def mod(v, n):
    return lax.rem(v + n, n)


def adasum_coefficients(gram):
    def get(m, i, j):
        return m[(i, j)] if i <= j else m[(j, i)]

    weights = [{i: None} for i in range(N)]
    count = N
    while count > 1:
        half = count // 2
        coef = []
        for i in range(half):
            cross = get(gram, 2 * i, 2 * i + 1)
            lower_sq = jnp.maximum(get(gram, 2 * i, 2 * i), 0.0)
            upper_sq = jnp.maximum(get(gram, 2 * i + 1, 2 * i + 1), 0.0)
            coef.append(
                (
                    1.0 - cross / (2.0 * (lower_sq + 1e-06)),
                    1.0 - cross / (2.0 * (upper_sq + 1e-06)),
                )
            )
        joined = []
        for i in range(half):
            node = {}
            for side in range(2):
                for leaf, w in weights[2 * i + side].items():
                    node[leaf] = coef[i][side] if w is None else w * coef[i][side]
            joined.append(node)
        weights = joined
        new_gram = {}
        for i in range(half):
            for j in range(i, half):
                total = None
                for a in range(2):
                    for b in range(2):
                        term = coef[i][a] * coef[j][b] * get(gram, 2 * i + a, 2 * j + b)
                        total = term if total is None else total + term
                new_gram[(i, j)] = total
        gram = new_gram
        count = half
    return [weights[0][i] for i in range(N)]


def kernel(
    scale,
    a_hbm, c_hbm, w_hbm, master_ref, momentum_ref,
    ig_ref, comb_ref, nw_ref,
    a_buf, c_buf, w_buf, part, r1a, r1b, r2a, r2b, fin, t_buf,
    gram_own, gram_x, gram_y, gram_g,
    load_a, load_c, load_w, rs_send, rs_recv, a2a_send, a2a_recv,
    gr_send, gr_recv, ag_send, ag_recv,
):
    grp = lax.axis_index("grp")
    sub = lax.axis_index("sub")
    z, c = grp // 2, lax.rem(grp, 2)
    y, x = sub // 4, lax.rem(sub, 4)

    def at_x(d):
        return (grp, y * 4 + mod(x + d, 4))

    def at_y(d):
        return (grp, mod(y + d, 4) * 4 + x)

    def at_z(d):
        return (mod(z + d, 4) * 2 + c, sub)

    def at_g(d):
        return (mod(grp + d, N), sub)

    along = {"x": (at_x, x), "y": (at_y, y), "z": (at_z, z)}
    other_core = (z * 2 + (1 - c), sub)

    def load_a_copy(k):
        col = pl.multiple_of(mod(grp + 1 + k, N) * 256, 256)
        return pltpu.make_async_copy(a_hbm.at[:, pl.ds(col, 256)], a_buf.at[k], load_a.at[k])

    def load_w_copy(k):
        return pltpu.make_async_copy(w_hbm.at[pl.ds(k * 256, 256)], w_buf.at[k], load_w.at[k])

    load_c_copy = pltpu.make_async_copy(c_hbm, c_buf, load_c)
    load_a_copy(0).start()
    load_c_copy.start()
    for k in range(1, N):
        load_a_copy(k).start()
    for k in range(N):
        load_w_copy(k).start()

    barrier = pltpu.get_barrier_semaphore()
    peers = [at_x(d) for d in (1, 2, 3)] + [at_y(d) for d in (1, 2, 3)]
    peers += [at_g(d) for d in range(1, N)]
    for peer in peers:
        pl.semaphore_signal(barrier, inc=1, device_id=peer, device_id_type=MESH)

    def remote(src, dst, send_sem, recv_sem, peer):
        return pltpu.make_async_remote_copy(
            src_ref=src, dst_ref=dst, send_sem=send_sem, recv_sem=recv_sem,
            device_id=peer, device_id_type=MESH,
        )

    halves = (
        (at_x, x, at_y, y),
        (at_y, y, at_x, x),
    )

    def rs_copy(stage, h, k, d):
        to1, me1, to2, me2 = halves[h]
        step = 1 if d == 0 else -1
        to = to1 if stage < 2 else to2
        if stage == 0:
            src = part.at[h, k, mod(me1 + 2, 4), pl.ds(2 * d, 2)]
            dst = r1a.at[h, k, d]
        elif stage == 1:
            src = part.at[h, k, mod(me1 + step, 4)]
            dst = r1b.at[h, k, d]
        elif stage == 2:
            src = part.at[h, k, me1, mod(me2 + 2, 4), pl.ds(8 * d, 8)]
            dst = r2a.at[h, k, d]
        else:
            src = part.at[h, k, me1, mod(me2 + step, 4)]
            dst = r2b.at[h, k, d]
        return remote(src, dst, rs_send.at[stage, h, k, d], rs_recv.at[stage, h, k, d], to(step))

    def a2a_copy(k):
        return remote(
            fin.at[k], t_buf.at[grp], a2a_send.at[k], a2a_recv.at[grp], at_g(1 + k)
        )

    def stage1(k):
        for h in range(2):
            for d in range(2):
                rs_copy(0, h, k, d).start()

    def stage2(k):
        for h in range(2):
            to1, me1, to2, me2 = halves[h]
            for d in range(2):
                step = 1 if d == 0 else -1
                rs_copy(0, h, k, d).wait_recv()
                mine = part.at[h, k, mod(me1 + step, 4), pl.ds(2 * d, 2)]
                mine[...] = mine[...] + r1a[h, k, d]
                rs_copy(1, h, k, d).start()

    def stage3(k):
        for h in range(2):
            to1, me1, to2, me2 = halves[h]
            rs_copy(1, h, k, 0).wait_recv()
            rs_copy(1, h, k, 1).wait_recv()
            mine = part.at[h, k, me1]
            mine[...] = mine[...] + (r1b[h, k, 0] + r1b[h, k, 1])
            for d in range(2):
                rs_copy(2, h, k, d).start()

    def stage4(k):
        for h in range(2):
            to1, me1, to2, me2 = halves[h]
            for d in range(2):
                step = 1 if d == 0 else -1
                rs_copy(2, h, k, d).wait_recv()
                mine = part.at[h, k, me1, mod(me2 + step, 4), pl.ds(8 * d, 8)]
                mine[...] = mine[...] + r2a[h, k, d]
                rs_copy(3, h, k, d).start()

    def stage5(k):
        for h in range(2):
            to1, me1, to2, me2 = halves[h]
            rs_copy(3, h, k, 0).wait_recv()
            rs_copy(3, h, k, 1).wait_recv()
            total = part[h, k, me1, me2] + (r2b[h, k, 0] + r2b[h, k, 1])
            fin[k, :, h * 512 : (h + 1) * 512] = total * scale

        @pl.when(k < N - 1)
        def _():
            a2a_copy(k).start()

    def weight_grad(k):
        load_a_copy(k).wait()
        left = a_buf[k]
        for h in range(2):
            res = lax.dot_general(
                left, c_buf[:, h * 512 : (h + 1) * 512],
                (((0,), (0,)), ((), ())), preferred_element_type=jnp.float32,
            )
            for yy in range(4):
                for xx in range(4):
                    row = (yy * 4 + xx) * 16
                    if h == 0:
                        part[h, k, xx, yy] = res[row : row + 16]
                    else:
                        part[h, k, yy, xx] = res[row : row + 16]

    def input_grad(k):
        load_w_copy(k).wait()
        res = lax.dot_general(
            c_buf[...], w_buf[k], (((1,), (1,)), ((), ())), preferred_element_type=jnp.float32
        )
        ig_ref[:, pl.ds(pl.multiple_of(k * 256, 256), 256)] = res.astype(jnp.bfloat16)

    load_c_copy.wait()

    def loop_body(t, carry):
        @pl.when(t < N)
        def _():
            weight_grad(t)

        @pl.when(t == 0)
        def _():
            pl.semaphore_wait(barrier, len(peers))

        @pl.when(t < N)
        def _():
            stage1(t)

        for lag, stage in ((LAG2, stage2), (LAG3, stage3), (LAG4, stage4), (LAG5, stage5)):

            @pl.when((t >= lag) & (t < N + lag))
            def _(lag=lag, stage=stage):
                stage(t - lag)

        @pl.when(t < N)
        def _():
            input_grad(t)

        return carry

    lax.fori_loop(0, N + LAG5, loop_body, 0)

    t_buf[grp] = fin[N - 1]
    for d in range(1, N):
        src = mod(grp + d, N)
        remote(fin.at[0], t_buf.at[src], a2a_send.at[0], a2a_recv.at[src], at_g(d)).wait_recv()

    def fold(v):
        acc = v[:, 0:128]
        for j in range(1, 8):
            acc = acc + v[:, j * 128 : (j + 1) * 128]
        return jnp.sum(acc, axis=0, keepdims=True)

    for n, (i, j) in enumerate(PAIRS):
        gram_own[pl.ds(n, 1), :] = fold(t_buf[i] * t_buf[j])
    gram_own[36:40, :] = jnp.zeros((4, 128), jnp.float32)

    base = 0
    rounds = ((at_x, 3, gram_x), (at_y, 3, gram_y), (at_g, 7, gram_g))
    for r, (to, count, slots) in enumerate(rounds):
        copies = [
            remote(gram_own.at[...] if r == 0 else rounds[r - 1][2].at[rounds[r - 1][1]],
                   slots.at[d - 1], gr_send.at[base + d - 1], gr_recv.at[base + d - 1], to(d))
            for d in range(1, count + 1)
        ]
        for cp in copies:
            cp.start()
        total = gram_own[...] if r == 0 else rounds[r - 1][2][rounds[r - 1][1]]
        for d, cp in enumerate(copies):
            cp.wait_recv()
        for d in range(count):
            total = total + slots[d]
        slots[count] = total
        base += count

    sums = jnp.sum(gram_g[7], axis=1, keepdims=True)
    gram = {pair: sums[n : n + 1, :] for n, pair in enumerate(PAIRS)}
    coef = adasum_coefficients(gram)
    combined = coef[0] * t_buf[0]
    for i in range(1, N):
        combined = combined + coef[i] * t_buf[i]
    comb_ref[...] = combined
    new_master = master_ref[...] - 0.05 * (0.9 * momentum_ref[...] + combined)
    nw_ref[z, c, y, x] = new_master.astype(jnp.bfloat16)

    def ag_region(p, fixed, core):
        col, width, _ = PARTS[p]
        idx = tuple(fixed.get(name, slice(None)) for name in "zyx")
        return nw_ref.at[idx[0], core, idx[1], idx[2], :, pl.ds(col, width)]

    me = {"x": x, "y": y, "z": z}

    def ag_copy(p, s, d, owner_off=0):
        order = PARTS[p][2]
        fixed = {name: mod(me[name] + (owner_off if name == order[s] else 0), 4)
                 for name in order[s:]}
        region = ag_region(p, fixed, c)
        n = (p * 3 + s) * 3 + d - 1
        return remote(region, region, ag_send.at[n], ag_recv.at[n], along[order[s]][0](d))

    def core_copy(p, j, core):
        order = PARTS[p][2]
        region = ag_region(p, {order[2]: mod(me[order[2]] + j, 4)}, core)
        n = 27 + p * 4 + j
        return remote(region, region, ag_send.at[n], ag_recv.at[n], other_core)

    for s in range(3):
        for p in range(3):
            if s > 0:
                for d in range(1, 4):
                    ag_copy(p, s - 1, d, -d).wait_recv()
            for d in range(1, 4):
                ag_copy(p, s, d).start()
            if s == 2:
                core_copy(p, 0, c).start()
    for d in (1, 3, 2):
        for p in range(3):
            ag_copy(p, 2, d, -d).wait_recv()
            core_copy(p, 4 - d, c).start()

    def drain(k, carry):
        for stage in range(4):
            for h in range(2):
                for d in range(2):
                    rs_copy(stage, h, k, d).wait_send()

        @pl.when(k < N - 1)
        def _():
            a2a_copy(k).wait_send()

        return carry

    lax.fori_loop(0, N, drain, 0)
    base = 0
    for r, (to, count, slots) in enumerate(rounds):
        for d in range(1, count + 1):
            remote(gram_own, slots.at[d - 1], gr_send.at[base + d - 1],
                   gr_recv.at[base + d - 1], to(d)).wait_send()
        base += count
    for p in range(3):
        for s in range(3):
            for d in range(1, 4):
                ag_copy(p, s, d).wait_send()
        for j in range(4):
            core_copy(p, j, c).wait_send()
            core_copy(p, j, 1 - c).wait_recv()


def body(activations, cotangent, weight, master, momentum):
    rows, width = activations.shape
    kv = cotangent.shape[1]
    scale = 1.0 / math.sqrt(rows * lax.axis_size("sub"))
    f32, bf16 = jnp.float32, jnp.bfloat16
    dma = pltpu.SemaphoreType.DMA
    vmem = pl.BlockSpec(memory_space=pltpu.VMEM)
    hbm = pl.BlockSpec(memory_space=pl.ANY)
    input_grad, combined, gathered = pl.pallas_call(
        functools.partial(kernel, scale),
        name="fused_step",
        in_specs=[hbm, hbm, hbm, vmem, vmem],
        out_specs=[vmem, vmem, vmem],
        out_shape=[
            pltpu.VMEM((rows, width), bf16),
            pltpu.VMEM((16, kv), f32),
            pltpu.VMEM((4, 2, 4, 4, 16, kv), bf16),
        ],
        scratch_shapes=[
            pltpu.VMEM((N, rows, 256), bf16),
            pltpu.VMEM((rows, kv), bf16),
            pltpu.VMEM((N, 256, kv), bf16),
            pltpu.VMEM((2, N, 4, 4, 16, 512), f32),
            pltpu.VMEM((2, N, 2, 2, 16, 512), f32),
            pltpu.VMEM((2, N, 2, 4, 16, 512), f32),
            pltpu.VMEM((2, N, 2, 8, 512), f32),
            pltpu.VMEM((2, N, 2, 16, 512), f32),
            pltpu.VMEM((N, 16, kv), f32),
            pltpu.VMEM((N, 16, kv), f32),
            pltpu.VMEM((40, 128), f32),
            pltpu.VMEM((4, 40, 128), f32),
            pltpu.VMEM((4, 40, 128), f32),
            pltpu.VMEM((8, 40, 128), f32),
            dma((N,)), dma, dma((N,)),
            dma((4, 2, N, 2)), dma((4, 2, N, 2)),
            dma((N,)), dma((N,)),
            dma((13,)), dma((13,)),
            dma((39,)), dma((39,)),
        ],
        compiler_params=pltpu.CompilerParams(
            collective_id=0, has_side_effects=True, vmem_limit_bytes=46 << 20
        ),
    )(activations, cotangent, weight, master, momentum)
    new_momentum = 0.9 * momentum + combined
    new_master = master - 0.05 * new_momentum
    return (input_grad, new_momentum, new_master, gathered.reshape(width, kv))


def solution(mesh):
    spec = P(("grp", "sub"), None)
    return jax.shard_map(
        body,
        mesh=mesh,
        in_specs=(spec, spec, P(), spec, spec),
        out_specs=(spec, spec, spec, P()),
        check_vma=False,
    )
```

```python
import functools
import math

import jax
import jax.numpy as jnp
from jax import lax
from jax.experimental import pallas as pl
from jax.experimental.pallas import tpu as pltpu
from jax.sharding import PartitionSpec as P

MESH = pl.DeviceIdType.MESH
N = 8
LAGS = (0, 2, 4, 6)
SECOND = 6
GRAM = (13, 15, 17, 19)
PARTS = ((0, 384, "yzx"), (384, 384, "xzy"), (768, 256, "xyz"))
PAIRS = [(i, j) for i in range(N) for j in range(i, N)]


def mod(v, n):
    return lax.rem(v + n, n)


def adasum_coefficients(gram):
    def get(m, i, j):
        return m[(i, j)] if i <= j else m[(j, i)]

    weights = [{i: None} for i in range(N)]
    count = N
    while count > 1:
        half = count // 2
        coef = []
        for i in range(half):
            cross = get(gram, 2 * i, 2 * i + 1)
            lower_sq = jnp.maximum(get(gram, 2 * i, 2 * i), 0.0)
            upper_sq = jnp.maximum(get(gram, 2 * i + 1, 2 * i + 1), 0.0)
            coef.append(
                (
                    1.0 - cross / (2.0 * (lower_sq + 1e-06)),
                    1.0 - cross / (2.0 * (upper_sq + 1e-06)),
                )
            )
        joined = []
        for i in range(half):
            node = {}
            for side in range(2):
                for leaf, w in weights[2 * i + side].items():
                    node[leaf] = coef[i][side] if w is None else w * coef[i][side]
            joined.append(node)
        weights = joined
        new_gram = {}
        for i in range(half):
            for j in range(i, half):
                total = None
                for a in range(2):
                    for b in range(2):
                        term = coef[i][a] * coef[j][b] * get(gram, 2 * i + a, 2 * j + b)
                        total = term if total is None else total + term
                new_gram[(i, j)] = total
        gram = new_gram
        count = half
    return [weights[0][i] for i in range(N)]


def kernel(
    scale,
    a_hbm, c_hbm, w_hbm, master_ref, momentum_ref,
    ig_ref, comb_ref, nw0, nw1, nw2,
    a_buf, c_buf, w_buf, part, out, r1a, r1b, r2, fin, t_buf,
    gram_own, gram_x, gram_y, gram_g,
    load_a, load_c, load_w, ring_send, ring_recv, direct_send, direct_recv, a2a_send, a2a_recv,
    gr_send, gr_recv, ag_send, ag_recv,
):
    grp = lax.axis_index("grp")
    sub = lax.axis_index("sub")
    z, c = grp // 2, lax.rem(grp, 2)
    y, x = sub // 4, lax.rem(sub, 4)

    def at_x(d):
        return (grp, y * 4 + mod(x + d, 4))

    def at_y(d):
        return (grp, mod(y + d, 4) * 4 + x)

    def at_z(d):
        return (mod(z + d, 4) * 2 + c, sub)

    def at_g(d):
        return (mod(grp + d, N), sub)

    along = {"x": (at_x, x), "y": (at_y, y), "z": (at_z, z)}
    other_core = (z * 2 + (1 - c), sub)

    def load_a_copy(k):
        col = pl.multiple_of(mod(grp + 1 + k, N) * 256, 256)
        return pltpu.make_async_copy(a_hbm.at[:, pl.ds(col, 256)], a_buf.at[k], load_a.at[k])

    def load_w_copy(k):
        return pltpu.make_async_copy(w_hbm.at[pl.ds(k * 256, 256)], w_buf.at[k], load_w.at[k])

    load_c_copy = pltpu.make_async_copy(c_hbm, c_buf, load_c)
    load_a_copy(0).start()
    load_c_copy.start()
    for k in range(1, N):
        load_a_copy(k).start()
    for k in range(N):
        load_w_copy(k).start()

    barrier = pltpu.get_barrier_semaphore()
    peers = [at_x(d) for d in (1, 2, 3)] + [at_y(d) for d in (1, 2, 3)]
    peers += [at_g(d) for d in range(1, N)]
    for peer in peers:
        pl.semaphore_signal(barrier, inc=1, device_id=peer, device_id_type=MESH)

    def remote(src, dst, send_sem, recv_sem, peer):
        return pltpu.make_async_remote_copy(
            src_ref=src, dst_ref=dst, send_sem=send_sem, recv_sem=recv_sem,
            device_id=peer, device_id_type=MESH,
        )

    halves = (
        (at_x, x, at_y, y),
        (at_y, y, at_x, x),
    )

    def ring_copy(q, stage, h, k, d):
        to1, me1, to2, me2 = halves[h]
        step = 1 if d == 0 else -1
        if stage == 0:
            src = out.at[q, h, k, mod(me1 + 2, 4), pl.ds(2 * d, 2)]
            dst = r1a.at[q, h, k, d]
        else:
            src = out.at[q, h, k, mod(me1 + step, 4)]
            dst = r1b.at[q, h, k, d]
        return remote(
            src, dst, ring_send.at[q, stage, h, k, d], ring_recv.at[q, stage, h, k, d], to1(step)
        )

    def direct_copy(q, h, k, d):
        to1, me1, to2, me2 = halves[h]
        return remote(
            out.at[q, h, k, me1, mod(me2 + d, 4)], r2.at[q, h, k, d - 1],
            direct_send.at[q, h, k, d - 1], direct_recv.at[q, h, k, d - 1], to2(d),
        )

    def a2a_copy(q, k):
        return remote(
            fin.at[q, k], t_buf.at[q, grp], a2a_send.at[q, k], a2a_recv.at[q, grp], at_g(1 + k)
        )

    def put(q, idx, value):
        rounded = value.astype(jnp.bfloat16)
        out[(q,) + idx] = rounded
        if q == 0:
            part[idx] = value - rounded.astype(jnp.float32)

    def wide(v):
        return v.astype(jnp.float32)

    def stage1(q, k):
        for h in range(2):
            to1, me1, to2, me2 = halves[h]
            idx = (h, k, mod(me1 + 2, 4))
            put(q, idx, part[idx])
            for d in range(2):
                ring_copy(q, 0, h, k, d).start()

    def stage2(q, k):
        for h in range(2):
            to1, me1, to2, me2 = halves[h]
            for d in range(2):
                step = 1 if d == 0 else -1
                far = (h, k, mod(me1 + step, 4), pl.ds(2 * (1 - d), 2))
                put(q, far, part[far])
                ring_copy(q, 0, h, k, d).wait_recv()
                near = (h, k, mod(me1 + step, 4), pl.ds(2 * d, 2))
                put(q, near, part[near] + wide(r1a[q, h, k, d]))
                ring_copy(q, 1, h, k, d).start()

    def stage3(q, k):
        for h in range(2):
            to1, me1, to2, me2 = halves[h]
            ring_copy(q, 1, h, k, 0).wait_recv()
            ring_copy(q, 1, h, k, 1).wait_recv()
            part[h, k, me1] = part[h, k, me1] + (wide(r1b[q, h, k, 0]) + wide(r1b[q, h, k, 1]))
            for d in (2, 1, 3):
                idx = (h, k, me1, mod(me2 + d, 4))
                put(q, idx, part[idx])
                direct_copy(q, h, k, d).start()

    def stage4(q, k):
        for h in range(2):
            to1, me1, to2, me2 = halves[h]
            total = part[h, k, me1, me2]
            for d in (1, 3, 2):
                direct_copy(q, h, k, d).wait_recv()
                total = total + wide(r2[q, h, k, d - 1])
            fin[q, k, :, h * 512 : (h + 1) * 512] = total * scale
            if q == 0:
                part[h, k, me1, me2] = jnp.zeros((16, 512), jnp.float32)

        @pl.when(k < N - 1)
        def _():
            a2a_copy(q, k).start()

    def arrived(q):
        t_buf[q, grp] = fin[q, N - 1]
        for d in range(1, N):
            src = mod(grp + d, N)
            remote(
                fin.at[q, 0], t_buf.at[q, src], a2a_send.at[q, 0], a2a_recv.at[q, src], at_g(d)
            ).wait_recv()

    def fold(v):
        acc = v[:, 0:128]
        for j in range(1, 8):
            acc = acc + v[:, j * 128 : (j + 1) * 128]
        return jnp.sum(acc, axis=0, keepdims=True)

    rounds = ((at_x, 3, gram_x), (at_y, 3, gram_y), (at_g, 7, gram_g))
    bases = (0, 3, 6)

    def gram_copy(r, d):
        to, count, slots = rounds[r]
        src = gram_own if r == 0 else rounds[r - 1][2].at[rounds[r - 1][1]]
        n = bases[r] + d - 1
        return remote(src, slots.at[d - 1], gr_send.at[n], gr_recv.at[n], to(d))

    def gram_products():
        arrived(0)
        for n, (i, j) in enumerate(PAIRS):
            gram_own[pl.ds(n, 1), :] = fold(t_buf[0, i] * t_buf[0, j])
        gram_own[36:40, :] = jnp.zeros((4, 128), jnp.float32)

    def gram_start(r):
        for d in range(1, rounds[r][1] + 1):
            gram_copy(r, d).start()

    def gram_sum(r):
        to, count, slots = rounds[r]
        total = gram_own[...] if r == 0 else rounds[r - 1][2][rounds[r - 1][1]]
        for d in range(1, count + 1):
            gram_copy(r, d).wait_recv()
            total = total + slots[d - 1]
        slots[count] = total

    def weight_grad(k):
        load_a_copy(k).wait()
        left = a_buf[k]
        for h in range(2):
            res = lax.dot_general(
                left, c_buf[:, h * 512 : (h + 1) * 512],
                (((0,), (0,)), ((), ())), preferred_element_type=jnp.float32,
            )
            for yy in range(4):
                for xx in range(4):
                    row = (yy * 4 + xx) * 16
                    if h == 0:
                        part[h, k, xx, yy] = res[row : row + 16]
                    else:
                        part[h, k, yy, xx] = res[row : row + 16]

    def input_grad(k):
        load_w_copy(k).wait()
        res = lax.dot_general(
            c_buf[...], w_buf[k], (((1,), (1,)), ((), ())), preferred_element_type=jnp.float32
        )
        ig_ref[:, pl.ds(pl.multiple_of(k * 256, 256), 256)] = res.astype(jnp.bfloat16)

    load_c_copy.wait()

    def loop_body(t, carry):
        @pl.when(t < N)
        def _():
            weight_grad(t)

        @pl.when(t == 0)
        def _():
            pl.semaphore_wait(barrier, len(peers))

        for q in range(2):
            for lag, stage in zip(LAGS, (stage1, stage2, stage3, stage4)):
                first = q * SECOND + lag

                @pl.when((t >= first) & (t < first + N))
                def _(q=q, first=first, stage=stage):
                    stage(q, t - first)

            if q == 0:
                for n, at in enumerate(GRAM):

                    @pl.when(t == at)
                    def _(n=n):
                        if n == 0:
                            gram_products()
                        else:
                            gram_sum(n - 1)
                        if n < 3:
                            gram_start(n)

        @pl.when((t >= N) & (t < 2 * N))
        def _():
            input_grad(t - N)

        return carry

    lax.fori_loop(0, max(SECOND + N + LAGS[3] - 1, GRAM[3]) + 1, loop_body, 0)
    arrived(1)

    sums = jnp.sum(gram_g[7], axis=1, keepdims=True)
    gram = {pair: sums[n : n + 1, :] for n, pair in enumerate(PAIRS)}
    coef = adasum_coefficients(gram)
    combined = coef[0] * (t_buf[0, 0] + t_buf[1, 0])
    for i in range(1, N):
        combined = combined + coef[i] * (t_buf[0, i] + t_buf[1, i])
    comb_ref[...] = combined
    new_master = master_ref[...] - 0.05 * (0.9 * momentum_ref[...] + combined)
    me = {"x": x, "y": y, "z": z}
    gathered = (nw0, nw1, nw2)
    updated = new_master.astype(jnp.bfloat16)
    for p, (col, width, order) in enumerate(PARTS):
        rest = [name for name in "zyx" if name != order[2]]
        gathered[p][c, me[order[2]], me[rest[0]], me[rest[1]]] = updated[:, col : col + width]

    def ag_region(p, fixed, core):
        last = PARTS[p][2][2]
        idx = [fixed.get(name, slice(None)) for name in "zyx" if name != last]
        return gathered[p].at[core, fixed[last], idx[0], idx[1]]

    def hop(p, s, d, back, piece=0):
        order = PARTS[p][2]
        fixed = {name: me[name] for name in order[s:]}
        if s == 2:
            fixed[order[1]] = mod(me[order[1]] + piece, 4)
        if back:
            fixed[order[s]] = mod(me[order[s]] - d, 4)
        region = ag_region(p, fixed, c)
        n = p * 18 + (s + piece) * 3 + d - 1
        return remote(region, region, ag_send.at[n], ag_recv.at[n], along[order[s]][0](d))

    def core_copy(p, j, core):
        order = PARTS[p][2]
        region = ag_region(p, {order[2]: mod(me[order[2]] + j, 4)}, core)
        n = 54 + p * 4 + j
        return remote(region, region, ag_send.at[n], ag_recv.at[n], other_core)

    near_first = (1, 3, 2)
    for p in range(3):
        for d in near_first:
            hop(p, 0, d, False).start()
    for p in range(3):
        for d in near_first:
            hop(p, 0, d, True).wait_recv()
        for d in near_first:
            hop(p, 1, d, False).start()
        for d in near_first:
            hop(p, 2, d, False).start()
    for piece in near_first:
        for p in range(3):
            hop(p, 1, 4 - piece, True).wait_recv()
            for d in near_first:
                hop(p, 2, d, False, piece).start()
    for p in range(3):
        core_copy(p, 0, c).start()
    for d in near_first:
        for p in range(3):
            for piece in range(4):
                hop(p, 2, d, True, piece).wait_recv()
            core_copy(p, 4 - d, c).start()

    def drain(k, carry):
        for q in range(2):
            for h in range(2):
                for d in range(2):
                    for stage in range(2):
                        ring_copy(q, stage, h, k, d).wait_send()
                for d in (1, 2, 3):
                    direct_copy(q, h, k, d).wait_send()

            @pl.when(k < N - 1)
            def _(q=q):
                a2a_copy(q, k).wait_send()

        return carry

    lax.fori_loop(0, N, drain, 0)
    for r in range(3):
        for d in range(1, rounds[r][1] + 1):
            gram_copy(r, d).wait_send()
    for p in range(3):
        for d in near_first:
            hop(p, 0, d, False).wait_send()
            hop(p, 1, d, False).wait_send()
            for piece in range(4):
                hop(p, 2, d, False, piece).wait_send()
        for j in range(4):
            core_copy(p, j, c).wait_send()
            core_copy(p, j, 1 - c).wait_recv()


def write_out(ig_ref, comb_ref, nw0, nw1, nw2, master_ref, momentum_ref,
              ig_out, momentum_out, master_out, nw_out, ig_sems, nw_sems):
    copies = []
    rows = ig_ref.shape[0] // 4
    for i in range(4):
        block = pl.ds(i * rows, rows)
        copies.append(pltpu.make_async_copy(ig_ref.at[block], ig_out.at[block], ig_sems.at[i]))
    for p, ((col, width, order), src) in enumerate(zip(PARTS, (nw0, nw1, nw2))):
        for core in range(2):
            for i in range(4):
                idx = [i if name == order[2] else slice(None) for name in "zyx"]
                dst = nw_out.at[idx[0], core, idx[1], idx[2], :, pl.ds(col, width)]
                copies.append(pltpu.make_async_copy(src.at[core, i], dst, nw_sems.at[p, core, i]))
    for copy in copies:
        copy.start()
    new_momentum = 0.9 * momentum_ref[...] + comb_ref[...]
    momentum_out[...] = new_momentum
    master_out[...] = master_ref[...] - 0.05 * new_momentum
    for copy in copies:
        copy.wait()


def body(activations, cotangent, weight, master, momentum):
    rows, width = activations.shape
    kv = cotangent.shape[1]
    scale = 1.0 / math.sqrt(rows * lax.axis_size("sub"))
    f32, bf16 = jnp.float32, jnp.bfloat16
    dma = pltpu.SemaphoreType.DMA
    vmem = pl.BlockSpec(memory_space=pltpu.VMEM)
    hbm = pl.BlockSpec(memory_space=pl.ANY)
    input_grad, combined, *gathered = pl.pallas_call(
        functools.partial(kernel, scale),
        name="fused_step",
        in_specs=[hbm, hbm, hbm, vmem, vmem],
        out_specs=[vmem] * 5,
        out_shape=[
            pltpu.VMEM((rows, width), bf16),
            pltpu.VMEM((16, kv), f32),
        ]
        + [pltpu.VMEM((2, 4, 4, 4, 16, wide), bf16) for _, wide, _ in PARTS],
        scratch_shapes=[
            pltpu.VMEM((N, rows, 256), bf16),
            pltpu.VMEM((rows, kv), bf16),
            pltpu.VMEM((N, 256, kv), bf16),
            pltpu.VMEM((2, N, 4, 4, 16, 512), f32),
            pltpu.VMEM((2, 2, N, 4, 4, 16, 512), bf16),
            pltpu.VMEM((2, 2, N, 2, 2, 16, 512), bf16),
            pltpu.VMEM((2, 2, N, 2, 4, 16, 512), bf16),
            pltpu.VMEM((2, 2, N, 3, 16, 512), bf16),
            pltpu.VMEM((2, N, 16, kv), f32),
            pltpu.VMEM((2, N, 16, kv), f32),
            pltpu.VMEM((40, 128), f32),
            pltpu.VMEM((4, 40, 128), f32),
            pltpu.VMEM((4, 40, 128), f32),
            pltpu.VMEM((8, 40, 128), f32),
            dma((N,)), dma, dma((N,)),
            dma((2, 2, 2, N, 2)), dma((2, 2, 2, N, 2)),
            dma((2, 2, N, 3)), dma((2, 2, N, 3)),
            dma((2, N)), dma((2, N)),
            dma((13,)), dma((13,)),
            dma((66,)), dma((66,)),
        ],
        compiler_params=pltpu.CompilerParams(
            collective_id=0, has_side_effects=True, vmem_limit_bytes=50 << 20
        ),
    )(activations, cotangent, weight, master, momentum)
    outs = pl.pallas_call(
        write_out,
        name="write_out",
        in_specs=[vmem] * 7,
        out_specs=[hbm, vmem, vmem, hbm],
        out_shape=[
            jax.ShapeDtypeStruct((rows, width), bf16),
            jax.ShapeDtypeStruct((16, kv), f32),
            jax.ShapeDtypeStruct((16, kv), f32),
            jax.ShapeDtypeStruct((4, 2, 4, 4, 16, kv), bf16),
        ],
        scratch_shapes=[dma((4,)), dma((3, 2, 4))],
        compiler_params=pltpu.CompilerParams(vmem_limit_bytes=2 << 20),
    )(input_grad, combined, *gathered, master, momentum)
    return (*outs[:3], outs[3].reshape(width, kv))


def solution(mesh):
    spec = P(("grp", "sub"), None)
    return jax.shard_map(
        body,
        mesh=mesh,
        in_specs=(spec, spec, P(), spec, spec),
        out_specs=(spec, spec, spec, P()),
        check_vma=False,
    )
```

```python
import functools
import math

import jax
import jax.numpy as jnp
from jax import lax
from jax.experimental import pallas as pl
from jax.experimental.pallas import tpu as pltpu
from jax.sharding import PartitionSpec as P

MESH = pl.DeviceIdType.MESH
N = 8
LAGS = (0, 2, 4, 6)
SECOND = 6
GRAM = (13, 15, 17, 19)
PARTS = ((0, 384, "yzx"), (384, 384, "xzy"), (768, 256, "xyz"))
PAIRS = [(i, j) for i in range(N) for j in range(i, N)]


def mod(v, n):
    return lax.rem(v + n, n)


def adasum_coefficients(gram):
    def get(m, i, j):
        return m[(i, j)] if i <= j else m[(j, i)]

    weights = [{i: None} for i in range(N)]
    count = N
    while count > 1:
        half = count // 2
        coef = []
        for i in range(half):
            cross = get(gram, 2 * i, 2 * i + 1)
            lower_sq = jnp.maximum(get(gram, 2 * i, 2 * i), 0.0)
            upper_sq = jnp.maximum(get(gram, 2 * i + 1, 2 * i + 1), 0.0)
            coef.append(
                (
                    1.0 - cross / (2.0 * (lower_sq + 1e-06)),
                    1.0 - cross / (2.0 * (upper_sq + 1e-06)),
                )
            )
        joined = []
        for i in range(half):
            node = {}
            for side in range(2):
                for leaf, w in weights[2 * i + side].items():
                    node[leaf] = coef[i][side] if w is None else w * coef[i][side]
            joined.append(node)
        weights = joined
        new_gram = {}
        for i in range(half):
            for j in range(i, half):
                total = None
                for a in range(2):
                    for b in range(2):
                        term = coef[i][a] * coef[j][b] * get(gram, 2 * i + a, 2 * j + b)
                        total = term if total is None else total + term
                new_gram[(i, j)] = total
        gram = new_gram
        count = half
    return [weights[0][i] for i in range(N)]


def kernel(
    scale,
    a_hbm, c_hbm, w_hbm, master_ref, momentum_ref,
    ig_ref, comb_ref, nw0, nw1, nw2,
    a_buf, c_buf, w_buf, part, out, r1a, r1b, r2, fin, t_buf,
    gram_own, gram_x, gram_y, gram_g,
    load_a, load_c, load_w, ring_send, ring_recv, direct_send, direct_recv, a2a_send, a2a_recv,
    gr_send, gr_recv, ag_send, ag_recv,
):
    grp = lax.axis_index("grp")
    sub = lax.axis_index("sub")
    z, c = grp // 2, lax.rem(grp, 2)
    y, x = sub // 4, lax.rem(sub, 4)

    def at_x(d):
        return (grp, y * 4 + mod(x + d, 4))

    def at_y(d):
        return (grp, mod(y + d, 4) * 4 + x)

    def at_z(d):
        return (mod(z + d, 4) * 2 + c, sub)

    def at_g(d):
        return (mod(grp + d, N), sub)

    along = {"x": (at_x, x), "y": (at_y, y), "z": (at_z, z)}
    other_core = (z * 2 + (1 - c), sub)

    def load_a_copy(k):
        col = pl.multiple_of(mod(grp + 1 + k, N) * 256, 256)
        return pltpu.make_async_copy(a_hbm.at[:, pl.ds(col, 256)], a_buf.at[k], load_a.at[k])

    def load_w_copy(k):
        return pltpu.make_async_copy(w_hbm.at[pl.ds(k * 256, 256)], w_buf.at[k], load_w.at[k])

    load_c_copy = pltpu.make_async_copy(c_hbm, c_buf, load_c)
    load_a_copy(0).start()
    load_c_copy.start()

    barrier = pltpu.get_barrier_semaphore()
    peers = [at_x(d) for d in (1, 2, 3)] + [at_y(d) for d in (1, 2, 3)]
    peers += [at_g(d) for d in range(1, N)]
    for peer in peers:
        pl.semaphore_signal(barrier, inc=1, device_id=peer, device_id_type=MESH)

    def remote(src, dst, send_sem, recv_sem, peer):
        return pltpu.make_async_remote_copy(
            src_ref=src, dst_ref=dst, send_sem=send_sem, recv_sem=recv_sem,
            device_id=peer, device_id_type=MESH,
        )

    halves = (
        (at_x, x, at_y, y),
        (at_y, y, at_x, x),
    )

    def ring_copy(q, stage, h, k, d):
        to1, me1, to2, me2 = halves[h]
        step = 1 if d == 0 else -1
        if stage == 0:
            src = out.at[q, h, k, mod(me1 + 2, 4), pl.ds(2 * d, 2)]
            dst = r1a.at[q, h, k, d]
        else:
            src = out.at[q, h, k, mod(me1 + step, 4)]
            dst = r1b.at[q, h, k, d]
        return remote(
            src, dst, ring_send.at[q, stage, h, k, d], ring_recv.at[q, stage, h, k, d], to1(step)
        )

    def direct_copy(q, h, k, d):
        to1, me1, to2, me2 = halves[h]
        return remote(
            out.at[q, h, k, me1, mod(me2 + d, 4)], r2.at[q, h, k, d - 1],
            direct_send.at[q, h, k, d - 1], direct_recv.at[q, h, k, d - 1], to2(d),
        )

    def a2a_copy(q, k):
        return remote(
            fin.at[q, k], t_buf.at[q, grp], a2a_send.at[q, k], a2a_recv.at[q, grp], at_g(1 + k)
        )

    def put(q, idx, value):
        rounded = value.astype(jnp.bfloat16)
        out[(q,) + idx] = rounded
        if q == 0:
            part[idx] = value - rounded.astype(jnp.float32)

    def wide(v):
        return v.astype(jnp.float32)

    def stage1(q, k):
        for h in range(2):
            to1, me1, to2, me2 = halves[h]
            idx = (h, k, mod(me1 + 2, 4))
            put(q, idx, part[idx])
            for d in range(2):
                ring_copy(q, 0, h, k, d).start()

    def stage2(q, k):
        for h in range(2):
            to1, me1, to2, me2 = halves[h]
            for d in range(2):
                step = 1 if d == 0 else -1
                far = (h, k, mod(me1 + step, 4), pl.ds(2 * (1 - d), 2))
                put(q, far, part[far])
                ring_copy(q, 0, h, k, d).wait_recv()
                near = (h, k, mod(me1 + step, 4), pl.ds(2 * d, 2))
                put(q, near, part[near] + wide(r1a[q, h, k, d]))
                ring_copy(q, 1, h, k, d).start()

    def stage3(q, k):
        for h in range(2):
            to1, me1, to2, me2 = halves[h]
            ring_copy(q, 1, h, k, 0).wait_recv()
            ring_copy(q, 1, h, k, 1).wait_recv()
            part[h, k, me1] = part[h, k, me1] + (wide(r1b[q, h, k, 0]) + wide(r1b[q, h, k, 1]))
            for d in (2, 1, 3):
                idx = (h, k, me1, mod(me2 + d, 4))
                put(q, idx, part[idx])
                direct_copy(q, h, k, d).start()

    def stage4(q, k):
        for h in range(2):
            to1, me1, to2, me2 = halves[h]
            total = part[h, k, me1, me2]
            for d in (1, 3, 2):
                direct_copy(q, h, k, d).wait_recv()
                total = total + wide(r2[q, h, k, d - 1])
            fin[q, k, :, h * 512 : (h + 1) * 512] = total * scale
            if q == 0:
                part[h, k, me1, me2] = jnp.zeros((16, 512), jnp.float32)

        @pl.when(k < N - 1)
        def _():
            a2a_copy(q, k).start()

    def arrived(q):
        t_buf[q, grp] = fin[q, N - 1]
        for d in range(1, N):
            src = mod(grp + d, N)
            remote(
                fin.at[q, 0], t_buf.at[q, src], a2a_send.at[q, 0], a2a_recv.at[q, src], at_g(d)
            ).wait_recv()

    def fold(v):
        acc = v[:, 0:128]
        for j in range(1, 8):
            acc = acc + v[:, j * 128 : (j + 1) * 128]
        return jnp.sum(acc, axis=0, keepdims=True)

    rounds = ((at_x, 3, gram_x), (at_y, 3, gram_y), (at_g, 7, gram_g))
    bases = (0, 3, 6)

    def gram_copy(r, d):
        to, count, slots = rounds[r]
        src = gram_own if r == 0 else rounds[r - 1][2].at[rounds[r - 1][1]]
        n = bases[r] + d - 1
        return remote(src, slots.at[d - 1], gr_send.at[n], gr_recv.at[n], to(d))

    def gram_products():
        arrived(0)
        for n, (i, j) in enumerate(PAIRS):
            gram_own[pl.ds(n, 1), :] = fold(t_buf[0, i] * t_buf[0, j])
        gram_own[36:40, :] = jnp.zeros((4, 128), jnp.float32)

    def gram_start(r):
        for d in range(1, rounds[r][1] + 1):
            gram_copy(r, d).start()

    def gram_sum(r):
        to, count, slots = rounds[r]
        total = gram_own[...] if r == 0 else rounds[r - 1][2][rounds[r - 1][1]]
        for d in range(1, count + 1):
            gram_copy(r, d).wait_recv()
            total = total + slots[d - 1]
        slots[count] = total

    def weight_grad(k):
        load_a_copy(k).wait()
        left = a_buf[k]
        for h in range(2):
            res = lax.dot_general(
                left, c_buf[:, h * 512 : (h + 1) * 512],
                (((0,), (0,)), ((), ())), preferred_element_type=jnp.float32,
            )
            for yy in range(4):
                for xx in range(4):
                    row = (yy * 4 + xx) * 16
                    if h == 0:
                        part[h, k, xx, yy] = res[row : row + 16]
                    else:
                        part[h, k, yy, xx] = res[row : row + 16]

    def input_grad(k):
        load_w_copy(k).wait()
        res = lax.dot_general(
            c_buf[...], w_buf[k], (((1,), (1,)), ((), ())), preferred_element_type=jnp.float32
        )
        ig_ref[:, pl.ds(pl.multiple_of(k * 256, 256), 256)] = res.astype(jnp.bfloat16)

    load_c_copy.wait()
    for k in range(1, N):
        load_a_copy(k).start()
    for k in range(N):
        load_w_copy(k).start()

    def loop_body(t, carry):
        @pl.when(t < N)
        def _():
            weight_grad(t)

        @pl.when(t == 0)
        def _():
            pl.semaphore_wait(barrier, len(peers))

        for q in range(2):
            for lag, stage in zip(LAGS, (stage1, stage2, stage3, stage4)):
                first = q * SECOND + lag

                @pl.when((t >= first) & (t < first + N))
                def _(q=q, first=first, stage=stage):
                    stage(q, t - first)

            if q == 0:
                for n, at in enumerate(GRAM):

                    @pl.when(t == at)
                    def _(n=n):
                        if n == 0:
                            gram_products()
                        else:
                            gram_sum(n - 1)
                        if n < 3:
                            gram_start(n)

        @pl.when((t >= N) & (t < 2 * N))
        def _():
            input_grad(t - N)

        return carry

    lax.fori_loop(0, max(SECOND + N + LAGS[3] - 1, GRAM[3]) + 1, loop_body, 0)
    arrived(1)

    sums = jnp.sum(gram_g[7], axis=1, keepdims=True)
    gram = {pair: sums[n : n + 1, :] for n, pair in enumerate(PAIRS)}
    coef = adasum_coefficients(gram)
    combined = coef[0] * (t_buf[0, 0] + t_buf[1, 0])
    for i in range(1, N):
        combined = combined + coef[i] * (t_buf[0, i] + t_buf[1, i])
    comb_ref[...] = combined
    new_master = master_ref[...] - 0.05 * (0.9 * momentum_ref[...] + combined)
    me = {"x": x, "y": y, "z": z}
    gathered = (nw0, nw1, nw2)
    updated = new_master.astype(jnp.bfloat16)
    for p, (col, width, order) in enumerate(PARTS):
        rest = [name for name in "zyx" if name != order[2]]
        gathered[p][c, me[order[2]], me[rest[0]], me[rest[1]]] = updated[:, col : col + width]

    def ag_region(p, fixed, core):
        last = PARTS[p][2][2]
        idx = [fixed.get(name, slice(None)) for name in "zyx" if name != last]
        return gathered[p].at[core, fixed[last], idx[0], idx[1]]

    def hop(p, s, d, back, piece=0):
        order = PARTS[p][2]
        fixed = {name: me[name] for name in order[s:]}
        if s == 2:
            fixed[order[1]] = mod(me[order[1]] + piece, 4)
        if back:
            fixed[order[s]] = mod(me[order[s]] - d, 4)
        region = ag_region(p, fixed, c)
        n = p * 18 + (s + piece) * 3 + d - 1
        return remote(region, region, ag_send.at[n], ag_recv.at[n], along[order[s]][0](d))

    def core_copy(p, j, core):
        order = PARTS[p][2]
        region = ag_region(p, {order[2]: mod(me[order[2]] + j, 4)}, core)
        n = 54 + p * 4 + j
        return remote(region, region, ag_send.at[n], ag_recv.at[n], other_core)

    near_first = (1, 3, 2)
    for p in range(3):
        for d in near_first:
            hop(p, 0, d, False).start()

    def drain(k, carry):
        for q in range(2):
            for h in range(2):
                for d in range(2):
                    for stage in range(2):
                        ring_copy(q, stage, h, k, d).wait_send()
                for d in (1, 2, 3):
                    direct_copy(q, h, k, d).wait_send()

            @pl.when(k < N - 1)
            def _(q=q):
                a2a_copy(q, k).wait_send()

        return carry

    lax.fori_loop(0, N, drain, 0)
    for r in range(3):
        for d in range(1, rounds[r][1] + 1):
            gram_copy(r, d).wait_send()

    for p in range(3):
        for d in near_first:
            hop(p, 0, d, True).wait_recv()
        for d in near_first:
            hop(p, 1, d, False).start()
        for d in near_first:
            hop(p, 2, d, False).start()
    for piece in near_first:
        for p in range(3):
            hop(p, 1, 4 - piece, True).wait_recv()
            for d in near_first:
                hop(p, 2, d, False, piece).start()
    for p in range(3):
        core_copy(p, 0, c).start()
        for d in near_first:
            hop(p, 0, d, False).wait_send()
            hop(p, 1, d, False).wait_send()
            hop(p, 2, d, False).wait_send()
    for d in near_first:
        for p in range(3):
            for piece in range(4):
                hop(p, 2, d, True, piece).wait_recv()
            core_copy(p, 4 - d, c).start()

    for p in range(3):
        for d in near_first:
            for piece in range(1, 4):
                hop(p, 2, d, False, piece).wait_send()
        for j in range(4):
            core_copy(p, j, c).wait_send()
            core_copy(p, j, 1 - c).wait_recv()


def write_out(ig_ref, comb_ref, nw0, nw1, nw2, master_ref, momentum_ref,
              ig_out, momentum_out, master_out, nw_out, ig_sems, nw_sems):
    copies = []
    rows = ig_ref.shape[0] // 4
    for i in range(4):
        block = pl.ds(i * rows, rows)
        copies.append(pltpu.make_async_copy(ig_ref.at[block], ig_out.at[block], ig_sems.at[i]))
    for p, ((col, width, order), src) in enumerate(zip(PARTS, (nw0, nw1, nw2))):
        for core in range(2):
            for i in range(4):
                idx = [i if name == order[2] else slice(None) for name in "zyx"]
                dst = nw_out.at[idx[0], core, idx[1], idx[2], :, pl.ds(col, width)]
                copies.append(pltpu.make_async_copy(src.at[core, i], dst, nw_sems.at[p, core, i]))
    for copy in copies:
        copy.start()
    new_momentum = 0.9 * momentum_ref[...] + comb_ref[...]
    momentum_out[...] = new_momentum
    master_out[...] = master_ref[...] - 0.05 * new_momentum
    for copy in copies:
        copy.wait()


def body(activations, cotangent, weight, master, momentum):
    rows, width = activations.shape
    kv = cotangent.shape[1]
    scale = 1.0 / math.sqrt(rows * lax.axis_size("sub"))
    f32, bf16 = jnp.float32, jnp.bfloat16
    dma = pltpu.SemaphoreType.DMA
    vmem = pl.BlockSpec(memory_space=pltpu.VMEM)
    hbm = pl.BlockSpec(memory_space=pl.ANY)
    input_grad, combined, *gathered = pl.pallas_call(
        functools.partial(kernel, scale),
        name="fused_step",
        in_specs=[hbm, hbm, hbm, vmem, vmem],
        out_specs=[vmem] * 5,
        out_shape=[
            pltpu.VMEM((rows, width), bf16),
            pltpu.VMEM((16, kv), f32),
        ]
        + [pltpu.VMEM((2, 4, 4, 4, 16, wide), bf16) for _, wide, _ in PARTS],
        scratch_shapes=[
            pltpu.VMEM((N, rows, 256), bf16),
            pltpu.VMEM((rows, kv), bf16),
            pltpu.VMEM((N, 256, kv), bf16),
            pltpu.VMEM((2, N, 4, 4, 16, 512), f32),
            pltpu.VMEM((2, 2, N, 4, 4, 16, 512), bf16),
            pltpu.VMEM((2, 2, N, 2, 2, 16, 512), bf16),
            pltpu.VMEM((2, 2, N, 2, 4, 16, 512), bf16),
            pltpu.VMEM((2, 2, N, 3, 16, 512), bf16),
            pltpu.VMEM((2, N, 16, kv), f32),
            pltpu.VMEM((2, N, 16, kv), f32),
            pltpu.VMEM((40, 128), f32),
            pltpu.VMEM((4, 40, 128), f32),
            pltpu.VMEM((4, 40, 128), f32),
            pltpu.VMEM((8, 40, 128), f32),
            dma((N,)), dma, dma((N,)),
            dma((2, 2, 2, N, 2)), dma((2, 2, 2, N, 2)),
            dma((2, 2, N, 3)), dma((2, 2, N, 3)),
            dma((2, N)), dma((2, N)),
            dma((13,)), dma((13,)),
            dma((66,)), dma((66,)),
        ],
        compiler_params=pltpu.CompilerParams(
            collective_id=0, has_side_effects=True, vmem_limit_bytes=50 << 20
        ),
    )(activations, cotangent, weight, master, momentum)
    outs = pl.pallas_call(
        write_out,
        name="write_out",
        in_specs=[vmem] * 7,
        out_specs=[hbm, vmem, vmem, hbm],
        out_shape=[
            jax.ShapeDtypeStruct((rows, width), bf16),
            jax.ShapeDtypeStruct((16, kv), f32),
            jax.ShapeDtypeStruct((16, kv), f32),
            jax.ShapeDtypeStruct((4, 2, 4, 4, 16, kv), bf16),
        ],
        scratch_shapes=[dma((4,)), dma((3, 2, 4))],
        compiler_params=pltpu.CompilerParams(vmem_limit_bytes=2 << 20),
    )(input_grad, combined, *gathered, master, momentum)
    return (*outs[:3], outs[3].reshape(width, kv))


def solution(mesh):
    spec = P(("grp", "sub"), None)
    return jax.shard_map(
        body,
        mesh=mesh,
        in_specs=(spec, spec, P(), spec, spec),
        out_specs=(spec, spec, spec, P()),
        check_vma=False,
    )
```

```python
import functools
import math

import jax
import jax.numpy as jnp
from jax import lax
from jax.experimental import pallas as pl
from jax.experimental.pallas import tpu as pltpu
from jax.sharding import PartitionSpec as P

MESH = pl.DeviceIdType.MESH
N = 8
LAGS = (0, 2, 4, 6)
SECOND = 6
GRAM = (13, 15, 17, 19)
PARTS = ((0, 384, "yzx"), (384, 384, "xzy"), (768, 256, "xyz"))
PAIRS = [(i, j) for i in range(N) for j in range(i, N)]


def mod(v, n):
    return lax.rem(v + n, n)


def adasum_coefficients(gram):
    def get(m, i, j):
        return m[(i, j)] if i <= j else m[(j, i)]

    weights = [{i: None} for i in range(N)]
    count = N
    while count > 1:
        half = count // 2
        coef = []
        for i in range(half):
            cross = get(gram, 2 * i, 2 * i + 1)
            lower_sq = jnp.maximum(get(gram, 2 * i, 2 * i), 0.0)
            upper_sq = jnp.maximum(get(gram, 2 * i + 1, 2 * i + 1), 0.0)
            coef.append(
                (
                    1.0 - cross / (2.0 * (lower_sq + 1e-06)),
                    1.0 - cross / (2.0 * (upper_sq + 1e-06)),
                )
            )
        joined = []
        for i in range(half):
            node = {}
            for side in range(2):
                for leaf, w in weights[2 * i + side].items():
                    node[leaf] = coef[i][side] if w is None else w * coef[i][side]
            joined.append(node)
        weights = joined
        new_gram = {}
        for i in range(half):
            for j in range(i, half):
                total = None
                for a in range(2):
                    for b in range(2):
                        term = coef[i][a] * coef[j][b] * get(gram, 2 * i + a, 2 * j + b)
                        total = term if total is None else total + term
                new_gram[(i, j)] = total
        gram = new_gram
        count = half
    return [weights[0][i] for i in range(N)]


def kernel(
    scale,
    a_hbm, c_hbm, w_hbm, master_ref, momentum_ref,
    ig_ref, comb_ref, nw0, nw1, nw2,
    a_buf, c_buf, w_buf, part, out, r1a, r1b, r2, fin, t_buf,
    gram_own, gram_x, gram_y, gram_g,
    load_a, load_c, load_w, ring_send, ring_recv, direct_send, direct_recv, a2a_send, a2a_recv,
    gr_send, gr_recv, ag_send, ag_recv,
):
    grp = lax.axis_index("grp")
    sub = lax.axis_index("sub")
    z, c = grp // 2, lax.rem(grp, 2)
    y, x = sub // 4, lax.rem(sub, 4)

    def at_x(d):
        return (grp, y * 4 + mod(x + d, 4))

    def at_y(d):
        return (grp, mod(y + d, 4) * 4 + x)

    def at_z(d):
        return (mod(z + d, 4) * 2 + c, sub)

    def at_g(d):
        return (mod(grp + d, N), sub)

    along = {"x": (at_x, x), "y": (at_y, y), "z": (at_z, z)}
    other_core = (z * 2 + (1 - c), sub)

    def load_a_copy(k):
        col = pl.multiple_of(mod(grp + 1 + k, N) * 256, 256)
        return pltpu.make_async_copy(a_hbm.at[:, pl.ds(col, 256)], a_buf.at[k], load_a.at[k])

    def load_w_copy(k):
        return pltpu.make_async_copy(w_hbm.at[pl.ds(k * 256, 256)], w_buf.at[k], load_w.at[k])

    load_c_copy = pltpu.make_async_copy(c_hbm, c_buf, load_c)
    load_a_copy(0).start()
    load_c_copy.start()

    barrier = pltpu.get_barrier_semaphore()
    peers = [at_x(d) for d in (1, 2, 3)] + [at_y(d) for d in (1, 2, 3)]
    peers += [at_g(d) for d in range(1, N)]
    for peer in peers:
        pl.semaphore_signal(barrier, inc=1, device_id=peer, device_id_type=MESH)

    def remote(src, dst, send_sem, recv_sem, peer):
        return pltpu.make_async_remote_copy(
            src_ref=src, dst_ref=dst, send_sem=send_sem, recv_sem=recv_sem,
            device_id=peer, device_id_type=MESH,
        )

    halves = (
        (at_x, x, at_y, y),
        (at_y, y, at_x, x),
    )

    def ring_copy(q, stage, h, k, d):
        to1, me1, to2, me2 = halves[h]
        step = 1 if d == 0 else -1
        if stage == 0:
            src = out.at[q, h, k, mod(me1 + 2, 4), pl.ds(2 * d, 2)]
            dst = r1a.at[q, h, k, d]
        else:
            src = out.at[q, h, k, mod(me1 + step, 4)]
            dst = r1b.at[q, h, k, d]
        return remote(
            src, dst, ring_send.at[q, stage, h, k, d], ring_recv.at[q, stage, h, k, d], to1(step)
        )

    def direct_copy(q, h, k, d):
        to1, me1, to2, me2 = halves[h]
        return remote(
            out.at[q, h, k, me1, mod(me2 + d, 4)], r2.at[q, h, k, d - 1],
            direct_send.at[q, h, k, d - 1], direct_recv.at[q, h, k, d - 1], to2(d),
        )

    def a2a_copy(q, k):
        return remote(
            fin.at[q, k], t_buf.at[q, grp], a2a_send.at[q, k], a2a_recv.at[q, grp], at_g(1 + k)
        )

    def put(q, idx, value):
        rounded = value.astype(jnp.bfloat16)
        out[(q,) + idx] = rounded
        if q == 0:
            part[idx] = value - rounded.astype(jnp.float32)

    def wide(v):
        return v.astype(jnp.float32)

    def stage1(q, k):
        for h in range(2):
            to1, me1, to2, me2 = halves[h]
            idx = (h, k, mod(me1 + 2, 4))
            put(q, idx, part[idx])
            for d in range(2):
                ring_copy(q, 0, h, k, d).start()

    def stage2(q, k):
        for h in range(2):
            to1, me1, to2, me2 = halves[h]
            for d in range(2):
                step = 1 if d == 0 else -1
                far = (h, k, mod(me1 + step, 4), pl.ds(2 * (1 - d), 2))
                put(q, far, part[far])
                ring_copy(q, 0, h, k, d).wait_recv()
                near = (h, k, mod(me1 + step, 4), pl.ds(2 * d, 2))
                put(q, near, part[near] + wide(r1a[q, h, k, d]))
                ring_copy(q, 1, h, k, d).start()

    def stage3(q, k):
        for h in range(2):
            to1, me1, to2, me2 = halves[h]
            ring_copy(q, 1, h, k, 0).wait_recv()
            ring_copy(q, 1, h, k, 1).wait_recv()
            part[h, k, me1] = part[h, k, me1] + (wide(r1b[q, h, k, 0]) + wide(r1b[q, h, k, 1]))
            for d in (2, 1, 3):
                idx = (h, k, me1, mod(me2 + d, 4))
                put(q, idx, part[idx])
                direct_copy(q, h, k, d).start()

    def stage4(q, k):
        for h in range(2):
            to1, me1, to2, me2 = halves[h]
            total = part[h, k, me1, me2]
            for d in (1, 3, 2):
                direct_copy(q, h, k, d).wait_recv()
                total = total + wide(r2[q, h, k, d - 1])
            fin[q, k, :, h * 512 : (h + 1) * 512] = total * scale
            if q == 0:
                part[h, k, me1, me2] = jnp.zeros((16, 512), jnp.float32)

        @pl.when(k < N - 1)
        def _():
            a2a_copy(q, k).start()

    def arrived(q):
        t_buf[q, grp] = fin[q, N - 1]
        for d in range(1, N):
            src = mod(grp + d, N)
            remote(
                fin.at[q, 0], t_buf.at[q, src], a2a_send.at[q, 0], a2a_recv.at[q, src], at_g(d)
            ).wait_recv()

    def fold(v):
        acc = v[:, 0:128]
        for j in range(1, 8):
            acc = acc + v[:, j * 128 : (j + 1) * 128]
        return jnp.sum(acc, axis=0, keepdims=True)

    rounds = ((at_x, 3, gram_x), (at_y, 3, gram_y), (at_g, 7, gram_g))
    bases = (0, 3, 6)

    def gram_copy(r, d):
        to, count, slots = rounds[r]
        src = gram_own if r == 0 else rounds[r - 1][2].at[rounds[r - 1][1]]
        n = bases[r] + d - 1
        return remote(src, slots.at[d - 1], gr_send.at[n], gr_recv.at[n], to(d))

    def gram_products():
        arrived(0)
        for n, (i, j) in enumerate(PAIRS):
            gram_own[pl.ds(n, 1), :] = fold(t_buf[0, i] * t_buf[0, j])
        gram_own[36:40, :] = jnp.zeros((4, 128), jnp.float32)

    def gram_start(r):
        for d in range(1, rounds[r][1] + 1):
            gram_copy(r, d).start()

    def gram_sum(r):
        to, count, slots = rounds[r]
        total = gram_own[...] if r == 0 else rounds[r - 1][2][rounds[r - 1][1]]
        for d in range(1, count + 1):
            gram_copy(r, d).wait_recv()
            total = total + slots[d - 1]
        slots[count] = total

    def weight_grad(k):
        load_a_copy(k).wait()
        left = a_buf[k]
        for h in range(2):
            res = lax.dot_general(
                left, c_buf[:, h * 512 : (h + 1) * 512],
                (((0,), (0,)), ((), ())), preferred_element_type=jnp.float32,
            )
            for yy in range(4):
                for xx in range(4):
                    row = (yy * 4 + xx) * 16
                    if h == 0:
                        part[h, k, xx, yy] = res[row : row + 16]
                    else:
                        part[h, k, yy, xx] = res[row : row + 16]

    def input_grad(k):
        load_w_copy(k).wait()
        res = lax.dot_general(
            c_buf[...], w_buf[k], (((1,), (1,)), ((), ())), preferred_element_type=jnp.float32
        )
        ig_ref[:, pl.ds(pl.multiple_of(k * 256, 256), 256)] = res.astype(jnp.bfloat16)

    load_c_copy.wait()
    for k in range(1, N):
        load_a_copy(k).start()
    for k in range(N):
        load_w_copy(k).start()

    def loop_body(t, carry):
        @pl.when(t < N)
        def _():
            weight_grad(t)

        @pl.when(t == 0)
        def _():
            pl.semaphore_wait(barrier, len(peers))

        for q in range(2):
            for lag, stage in zip(LAGS, (stage1, stage2, stage3, stage4)):
                first = q * SECOND + lag

                @pl.when((t >= first) & (t < first + N))
                def _(q=q, first=first, stage=stage):
                    stage(q, t - first)

            if q == 0:
                for n, at in enumerate(GRAM):

                    @pl.when(t == at)
                    def _(n=n):
                        if n == 0:
                            gram_products()
                        else:
                            gram_sum(n - 1)
                        if n < 3:
                            gram_start(n)

        @pl.when((t >= N) & (t < 2 * N))
        def _():
            input_grad(t - N)

        return carry

    lax.fori_loop(0, max(SECOND + N + LAGS[3] - 1, GRAM[3]) + 1, loop_body, 0)
    arrived(1)

    sums = jnp.sum(gram_g[7], axis=1, keepdims=True)
    gram = {pair: sums[n : n + 1, :] for n, pair in enumerate(PAIRS)}
    coef = adasum_coefficients(gram)
    combined = coef[0] * (t_buf[0, 0] + t_buf[1, 0])
    for i in range(1, N):
        combined = combined + coef[i] * (t_buf[0, i] + t_buf[1, i])
    comb_ref[...] = combined
    new_master = master_ref[...] - 0.05 * (0.9 * momentum_ref[...] + combined)
    me = {"x": x, "y": y, "z": z}
    gathered = (nw0, nw1, nw2)
    updated = new_master.astype(jnp.bfloat16)
    for p, (col, width, order) in enumerate(PARTS):
        rest = [name for name in "zyx" if name != order[2]]
        gathered[p][c, me[order[2]], me[rest[0]], me[rest[1]]] = updated[:, col : col + width]

    def ag_region(p, fixed, core):
        last = PARTS[p][2][2]
        idx = [fixed.get(name, slice(None)) for name in "zyx" if name != last]
        return gathered[p].at[core, fixed[last], idx[0], idx[1]]

    def hop(p, s, d, back, piece=0):
        order = PARTS[p][2]
        fixed = {name: me[name] for name in order[s:]}
        if s == 2:
            fixed[order[1]] = mod(me[order[1]] + piece, 4)
        if back:
            fixed[order[s]] = mod(me[order[s]] - d, 4)
        region = ag_region(p, fixed, c)
        n = p * 18 + (s + piece) * 3 + d - 1
        return remote(region, region, ag_send.at[n], ag_recv.at[n], along[order[s]][0](d))

    def core_copy(p, core, d=0, piece=0):
        order = PARTS[p][2]
        fixed = {order[2]: mod(me[order[2]] - d, 4)}
        if d:
            fixed[order[1]] = mod(me[order[1]] + piece, 4)
        region = ag_region(p, fixed, core)
        n = 54 + p * 13 + (piece * 3 + d if d else 0)
        return remote(region, region, ag_send.at[n], ag_recv.at[n], other_core)

    near_first = (1, 3, 2)
    for p in range(3):
        for d in near_first:
            hop(p, 0, d, False).start()

    def drain(k, carry):
        for q in range(2):
            for h in range(2):
                for d in range(2):
                    for stage in range(2):
                        ring_copy(q, stage, h, k, d).wait_send()
                for d in (1, 2, 3):
                    direct_copy(q, h, k, d).wait_send()

            @pl.when(k < N - 1)
            def _(q=q):
                a2a_copy(q, k).wait_send()

        return carry

    lax.fori_loop(0, N, drain, 0)
    for r in range(3):
        for d in range(1, rounds[r][1] + 1):
            gram_copy(r, d).wait_send()

    for p in range(3):
        for d in near_first:
            hop(p, 0, d, True).wait_recv()
        for d in near_first:
            hop(p, 1, d, False).start()
        for d in near_first:
            hop(p, 2, d, False).start()
    for piece in near_first:
        for p in range(3):
            hop(p, 1, 4 - piece, True).wait_recv()
            for d in near_first:
                hop(p, 2, d, False, piece).start()
    for p in range(3):
        core_copy(p, c).start()
        for d in near_first:
            hop(p, 0, d, False).wait_send()
            hop(p, 1, d, False).wait_send()
            hop(p, 2, d, False).wait_send()
    for piece in (0,) + near_first:
        for p in range(3):
            for d in near_first:
                hop(p, 2, d, True, piece).wait_recv()
                core_copy(p, c, d, piece).start()

    for p in range(3):
        for d in near_first:
            for piece in range(1, 4):
                hop(p, 2, d, False, piece).wait_send()
        core_copy(p, c).wait_send()
        core_copy(p, 1 - c).wait_recv()
        for d in near_first:
            for piece in range(4):
                core_copy(p, c, d, piece).wait_send()
                core_copy(p, 1 - c, d, piece).wait_recv()


def write_out(ig_ref, comb_ref, nw0, nw1, nw2, master_ref, momentum_ref,
              ig_out, momentum_out, master_out, nw_out, ig_sems, nw_sems):
    copies = []
    rows = ig_ref.shape[0] // 4
    for i in range(4):
        block = pl.ds(i * rows, rows)
        copies.append(pltpu.make_async_copy(ig_ref.at[block], ig_out.at[block], ig_sems.at[i]))
    for p, ((col, width, order), src) in enumerate(zip(PARTS, (nw0, nw1, nw2))):
        for core in range(2):
            for i in range(4):
                idx = [i if name == order[2] else slice(None) for name in "zyx"]
                dst = nw_out.at[idx[0], core, idx[1], idx[2], :, pl.ds(col, width)]
                copies.append(pltpu.make_async_copy(src.at[core, i], dst, nw_sems.at[p, core, i]))
    for copy in copies:
        copy.start()
    new_momentum = 0.9 * momentum_ref[...] + comb_ref[...]
    momentum_out[...] = new_momentum
    master_out[...] = master_ref[...] - 0.05 * new_momentum
    for copy in copies:
        copy.wait()


def body(activations, cotangent, weight, master, momentum):
    rows, width = activations.shape
    kv = cotangent.shape[1]
    scale = 1.0 / math.sqrt(rows * lax.axis_size("sub"))
    f32, bf16 = jnp.float32, jnp.bfloat16
    dma = pltpu.SemaphoreType.DMA
    vmem = pl.BlockSpec(memory_space=pltpu.VMEM)
    hbm = pl.BlockSpec(memory_space=pl.ANY)
    input_grad, combined, *gathered = pl.pallas_call(
        functools.partial(kernel, scale),
        name="fused_step",
        in_specs=[hbm, hbm, hbm, vmem, vmem],
        out_specs=[vmem] * 5,
        out_shape=[
            pltpu.VMEM((rows, width), bf16),
            pltpu.VMEM((16, kv), f32),
        ]
        + [pltpu.VMEM((2, 4, 4, 4, 16, wide), bf16) for _, wide, _ in PARTS],
        scratch_shapes=[
            pltpu.VMEM((N, rows, 256), bf16),
            pltpu.VMEM((rows, kv), bf16),
            pltpu.VMEM((N, 256, kv), bf16),
            pltpu.VMEM((2, N, 4, 4, 16, 512), f32),
            pltpu.VMEM((2, 2, N, 4, 4, 16, 512), bf16),
            pltpu.VMEM((2, 2, N, 2, 2, 16, 512), bf16),
            pltpu.VMEM((2, 2, N, 2, 4, 16, 512), bf16),
            pltpu.VMEM((2, 2, N, 3, 16, 512), bf16),
            pltpu.VMEM((2, N, 16, kv), f32),
            pltpu.VMEM((2, N, 16, kv), f32),
            pltpu.VMEM((40, 128), f32),
            pltpu.VMEM((4, 40, 128), f32),
            pltpu.VMEM((4, 40, 128), f32),
            pltpu.VMEM((8, 40, 128), f32),
            dma((N,)), dma, dma((N,)),
            dma((2, 2, 2, N, 2)), dma((2, 2, 2, N, 2)),
            dma((2, 2, N, 3)), dma((2, 2, N, 3)),
            dma((2, N)), dma((2, N)),
            dma((13,)), dma((13,)),
            dma((93,)), dma((93,)),
        ],
        compiler_params=pltpu.CompilerParams(
            collective_id=0, has_side_effects=True, vmem_limit_bytes=50 << 20
        ),
    )(activations, cotangent, weight, master, momentum)
    outs = pl.pallas_call(
        write_out,
        name="write_out",
        in_specs=[vmem] * 7,
        out_specs=[hbm, vmem, vmem, hbm],
        out_shape=[
            jax.ShapeDtypeStruct((rows, width), bf16),
            jax.ShapeDtypeStruct((16, kv), f32),
            jax.ShapeDtypeStruct((16, kv), f32),
            jax.ShapeDtypeStruct((4, 2, 4, 4, 16, kv), bf16),
        ],
        scratch_shapes=[dma((4,)), dma((3, 2, 4))],
        compiler_params=pltpu.CompilerParams(vmem_limit_bytes=2 << 20),
    )(input_grad, combined, *gathered, master, momentum)
    return (*outs[:3], outs[3].reshape(width, kv))


def solution(mesh):
    spec = P(("grp", "sub"), None)
    return jax.shard_map(
        body,
        mesh=mesh,
        in_specs=(spec, spec, P(), spec, spec),
        out_specs=(spec, spec, spec, P()),
        check_vma=False,
    )
```
